128 devices in a mesh: exp: 8 (over x, core), fsdp: 16 (over z, y).
Axes of the slice: x: 4, y: 4, z: 4, core: 2. Of those that a mesh axis runs over, the one named last changes fastest.
Arguments:
- tokens: bfloat16 [16384, 1536], P(('exp', 'fsdp')), may hold values from -6 to 6
- expert_ids: int32 [16384, 2], P(('exp', 'fsdp')), may hold values from 0 to 7, all different within a row; in each aligned block of 128 rows (0 to 127, 128 to 255, ...) at most 48 rows name the same one
- gates: float32 [16384, 2], P(('exp', 'fsdp')), may hold values from 0.1 to 1
- w_in: bfloat16 [8, 2048, 1536], P('exp', 'fsdp'), may hold values from -0.15625 to 0.15625
- w_out: bfloat16 [8, 2048, 1536], P('exp', 'fsdp'), may hold values from -0.125 to 0.125
- grad_y: bfloat16 [16384, 1536], P(('exp', 'fsdp')), may hold values from -6 to 6
Outputs:
- mixed: bfloat16 [16384, 1536], P(('exp', 'fsdp'))
- grad_tokens: bfloat16 [16384, 1536], P(('exp', 'fsdp'))
- grad_w_in: float32 [8, 2048, 1536], P('exp', 'fsdp')
- grad_w_out: float32 [8, 2048, 1536], P('exp', 'fsdp')
- grad_gates: float32 [16384, 2], P(('exp', 'fsdp'))
The draws below stay inside these ranges and needn't reach their ends.
Inputs may be any that keep to these rules, and one draw needn't show every extreme that they name: `expert_ids`: each row names two different experts. Among the rows of one device no expert is named by more than 48 rows, and in some device some expert is named by exactly 48 rows.
All inputs are finite; a program needn't handle non-finite values.
Results may differ from the reference program's by a relative error of at most 0.0065.
Values may be sent and summed in bfloat16 or wider, within the bound.
A program may use at most 192 MiB of HBM per device.

```python
import math
import jax
import jax.numpy as jnp
import numpy as np
from jax import lax

D = 1536
H = 2048
TOK_DEV = 128
EXPERTS = 8
CAP = 48
TOKENS = 16384
N_EXP = 8
N_FSDP = 16


def level_of(own_key, shape, shards, low, top_value):
    def one(position, parts):
        steps = jax.random.uniform(jax.random.fold_in(jax.random.fold_in(own_key, 6), position), (parts,), jnp.float32, low / len(shards), top_value / len(shards))
        return jnp.repeat(jnp.exp(steps), shape[position] // parts).reshape((-1,) + (1,) * (len(shape) - position - 1))

    factor_of = one(*shards[0])
    for cut in shards[1:]:
        factor_of = factor_of * one(*cut)
    return factor_of


def routed_block(rng, own, number, rows, number_of, top, limit, skew):
    ranking = jax.random.permutation(rng, number_of)
    heavy_load, usual = shares(number_of, rows * top, limit, skew, True), shares(number_of, rows * top, limit, skew, False)
    places = jnp.arange(number_of)

    def named(sizes, offset_by):
        used = int((sizes > 0).sum())
        fixed = max(1, used // 4)
        moved = fixed + (places - fixed + offset_by * (used - fixed)) % max(1, number_of - fixed)
        return jnp.zeros((number_of,), jnp.int32).at[ranking[jnp.where(places < fixed, places, moved)]].set(jnp.asarray(sizes, jnp.int32))

    sizes = jnp.where(number % 4 == 0, named(heavy_load, number // 4), named(usual, number - number // 4 - 1))
    mixed = jax.random.permutation(jax.random.fold_in(own, 3), number_of)
    source_of, taker = mixed[0:number_of // 2 * 2:2], mixed[1:number_of // 2 * 2:2]
    room = jnp.minimum(sizes[source_of] - 1, limit - sizes[taker]) // 2
    room = jnp.where((source_of == ranking[0]) | (taker == ranking[0]) | (sizes[taker] == 0), 0, jnp.maximum(room, 0))
    moved = jax.random.randint(jax.random.fold_in(own, 4), (number_of // 2,), 0, 1 << 20) % (room + 1)
    sizes = sizes.at[source_of].add(-moved).at[taker].add(moved)
    members = jnp.searchsorted(jnp.cumsum(sizes), jnp.arange(rows * top), side="right").astype(jnp.int32)
    listing = members.reshape(top, rows).T
    listing = listing[jax.random.permutation(jax.random.fold_in(own, 1), rows)]
    offset_by = jax.random.randint(jax.random.fold_in(own, 2), (rows, 1), 0, top)
    return jnp.take_along_axis(listing, (jnp.arange(top)[None, :] + offset_by) % top, axis=1)


def shares(amount, total, reach, lean, full):
    weights = [(1 << 20) // math.isqrt(grade ** lean) + 1 for grade in range(1, amount + 1)]
    largest = reach if full else min(reach, max(-(-total // amount), total * weights[0] // sum(weights)))
    least = 1 if total - largest >= amount - 1 else 0
    counts, surplus = [largest] + [least] * (amount - 1), total - largest - least * (amount - 1)
    while surplus > 0:
        free = [i for i in range(1, amount) if counts[i] < largest] or [i for i in range(1, amount) if counts[i] < reach]
        pool, budget = sum([weights[i] for i in free]), surplus
        for i in free:
            extra = min(reach - counts[i], max(1, budget * weights[i] // pool), surplus)
            counts[i] = counts[i] + extra
            surplus = surplus - extra
    return np.array(counts)


def centred(own_key, shape, width, bound, cuts=(), held_as=jnp.bfloat16):
    array = jax.random.normal(own_key, shape, jnp.float32) * width
    if len(cuts) > 0:
        array = level_of(own_key, shape, cuts, -0.22, 0.18) * array
    return jnp.clip(array, min=-bound, max=bound).astype(held_as)


def setup_inputs(seed: int = 0) -> dict:
    key_list = jax.random.split(jax.random.key(seed), 7)
    tokens = centred(key_list[0], (TOKENS, D), 1.0, 6.0, ((0, 128),))
    expert_ids_keys = jax.random.split(jax.random.fold_in(key_list[1], 1), TOKENS // TOK_DEV)
    expert_ids_turns = jax.random.permutation(jax.random.fold_in(key_list[1], 3), TOKENS // TOK_DEV)
    expert_ids = jax.vmap(lambda own, number: routed_block(jax.random.fold_in(key_list[1], 2), own, number, TOK_DEV, EXPERTS, 2, CAP, 1))(expert_ids_keys, expert_ids_turns).reshape((TOKENS, 2))
    gates = jnp.clip(0.1 + 0.9 * jax.random.uniform(key_list[2], (TOKENS, 2), jnp.float32) ** level_of(key_list[2], (TOKENS, 2), ((0, 128),), -0.2, 0.2), 0.1, 1.0)
    w_in = centred(key_list[3], (EXPERTS, H, D), D ** -0.5, 0.15625, ((0, 8), (1, 16)))
    w_out = centred(key_list[4], (EXPERTS, H, D), H ** -0.5, 0.125, ((0, 8), (1, 16)))
    grad_y = centred(key_list[5], (TOKENS, D), 1.0, 6.0, ((0, 128),))
    return dict(tokens=tokens, expert_ids=expert_ids, gates=gates, w_in=w_in, w_out=w_out, grad_y=grad_y)


inv_sqrt_two = 0.7071067811865476
inv_sqrt_two_pi = 0.3989422804014327

def gelu_parts(values):
    cdf_part = 0.5 * (1.0 + jax.scipy.special.erf(values * inv_sqrt_two))
    return (values * cdf_part, cdf_part + values * jnp.exp(-0.5 * values * values) * inv_sqrt_two_pi)

def contract_first(left, right):
    return lax.dot_general(left, right, (((0,), (0,)), ((), ())), preferred_element_type=jnp.float32)

def contract_last(left, right):
    return lax.dot_general(left, right, (((1,), (1,)), ((), ())), preferred_element_type=jnp.float32)

def reference(tokens, expert_ids, gates, w_in, w_out, grad_y):
    flat_ids = expert_ids.reshape(-1).astype(jnp.int32)
    slot_total = flat_ids.shape[0]
    row_limit = N_EXP * N_FSDP * CAP
    slot_grad = (gates[:, :, None] * grad_y.astype(jnp.float32)[:, None, :]).astype(jnp.bfloat16)
    slot_grad = slot_grad.reshape(slot_total, D)

    def per_expert(carry, expert):
        out_slots, input_slots = carry
        row_index = jnp.nonzero(flat_ids == expert, size=row_limit, fill_value=slot_total)[0].astype(jnp.int32)
        is_live = row_index < slot_total
        safe_index = jnp.where(is_live, row_index, 0).astype(jnp.int32)
        rows_in = jnp.where(is_live[:, None], tokens[safe_index // 2], jnp.zeros((), jnp.bfloat16))
        grad_rows = jnp.where(is_live[:, None], slot_grad[safe_index], jnp.zeros((), jnp.bfloat16))
        weight_in = lax.dynamic_index_in_dim(w_in, expert, 0, keepdims=False)
        weight_out = lax.dynamic_index_in_dim(w_out, expert, 0, keepdims=False)
        hidden_pre = contract_last(rows_in, weight_in)
        act_full, slope_term = gelu_parts(hidden_pre)
        act_bf = act_full.astype(jnp.bfloat16)
        expert_out = jnp.dot(act_bf, weight_out, preferred_element_type=jnp.float32).astype(jnp.bfloat16)
        grad_act = contract_last(grad_rows, weight_out)
        grad_hidden = (grad_act * slope_term).astype(jnp.bfloat16)
        input_grad = jnp.dot(grad_hidden, weight_in, preferred_element_type=jnp.float32).astype(jnp.bfloat16)
        grad_in = contract_first(grad_hidden, rows_in)
        grad_out = contract_first(act_bf, grad_rows)
        out_slots = out_slots.at[row_index].set(expert_out, mode='drop')
        input_slots = input_slots.at[row_index].set(input_grad, mode='drop')
        return ((out_slots, input_slots), (grad_in, grad_out))
    start_carry = (jnp.zeros((slot_total, D), jnp.bfloat16), jnp.zeros((slot_total, D), jnp.bfloat16))
    (out_slots, input_slots), (grad_w_in, grad_w_out) = lax.scan(per_expert, start_carry, jnp.arange(EXPERTS, dtype=jnp.int32))
    out_three = out_slots.reshape(TOKENS, 2, D).astype(jnp.float32)
    mixed = lax.optimization_barrier(jnp.sum(gates[:, :, None] * out_three, axis=1)).astype(jnp.bfloat16)
    grad_gates = lax.optimization_barrier(jnp.sum(grad_y.astype(jnp.float32)[:, None, :] * out_three, axis=-1))
    grad_tokens = lax.optimization_barrier(jnp.sum(input_slots.reshape(TOKENS, 2, D).astype(jnp.float32), axis=1)).astype(jnp.bfloat16)
    return (mixed, grad_tokens, grad_w_in, grad_w_out, grad_gates)
```

```python
import functools

import jax
import jax.numpy as jnp
from jax import lax
from jax.experimental import pallas as pl
from jax.experimental.pallas import tpu as pltpu
from jax.sharding import PartitionSpec as P

inv_sqrt_two = 0.7071067811865476
inv_sqrt_two_pi = 0.3989422804014327
MESH = pl.DeviceIdType.MESH
SIDE = 4
BF = jnp.bfloat16
F32 = jnp.float32


def dot(left, right, over):
    return lax.dot_general(left, right, (over, ((), ())), preferred_element_type=F32)


def kernel(
    experts,
    ids_row,
    gates_row,
    gates_col,
    tokens,
    grad_y,
    w_in,
    w_out,
    mixed,
    grad_tokens,
    grad_in,
    grad_out,
    grad_gates,
    wts,
    parts,
    relay1,
    full1,
    relay2,
    full2,
    sendx,
    recvx,
    backx,
    acc,
    act_s,
    gh_s,
    act_t,
    gh_t,
    load_sem,
    ag_send,
    ag_recv,
    rs_send,
    rs_recv,
    x_send,
    x_recv,
):
    rows, features = tokens.shape
    half = w_in.shape[0] // 2
    cap = sendx.shape[2]
    slots = experts * cap
    group = SIDE * half
    tile = features // 3

    e = lax.axis_index("exp")
    f = lax.axis_index("fsdp")
    z, y = f // SIDE, f % SIDE

    def ring(value):
        return (value + SIDE) % SIDE

    first, second = (y, z), (z, y)

    def peer(h, second_axis, step):
        along_z = (h == 0) == second_axis
        nz = ring(z + step) if along_z else z
        ny = y if along_z else ring(y + step)
        return (e, nz * SIDE + ny)

    def copy(src, dst, send, recv, to):
        return pltpu.make_async_remote_copy(
            src_ref=src, dst_ref=dst, send_sem=send, recv_sem=recv, device_id=to, device_id_type=MESH
        )

    def gather_region(h, i, k, sent):
        a, b = first[h], second[h]
        if i is None:
            if sent:
                return (wts.at[h, a, b], wts.at[h, a, b], wts.at[h, ring(a - 1), b, 0], wts.at[h, ring(a + 1), b, 1])[k]
            return (
                wts.at[h, ring(a - 1), b],
                wts.at[h, ring(a + 1), b],
                wts.at[h, ring(a + 2), b, 0],
                wts.at[h, ring(a + 2), b, 1],
            )[k]
        g = ring(a - i)
        if sent:
            return (wts.at[h, g, b], wts.at[h, g, b], wts.at[h, g, ring(b - 1), 0], wts.at[h, g, ring(b + 1), 1])[k]
        return (
            wts.at[h, g, ring(b - 1)],
            wts.at[h, g, ring(b + 1)],
            wts.at[h, g, ring(b + 2), 0],
            wts.at[h, g, ring(b + 2), 1],
        )[k]

    def gather(h, i, k, sent=True):
        region = gather_region(h, i, k, sent)
        s = k if i is None else 4 + 4 * i + k
        step = 1 if k % 2 == 0 else -1
        return copy(region, region, ag_send.at[h, s], ag_recv.at[h, s], peer(h, i is not None, step))

    def got(h, i, k):
        gather(h, i, k, sent=False).wait_recv()

    def reduce1(h, i, k):
        a, b = first[h], second[h]
        g = ring(a - i)
        src = (
            parts.at[h, g, ring(b + 2), 0],
            parts.at[h, g, ring(b + 2), 1],
            parts.at[h, g, ring(b + 1)],
            parts.at[h, g, ring(b - 1)],
        )[k]
        dst = (relay1.at[h, i, 0], relay1.at[h, i, 1], full1.at[h, i, 0], full1.at[h, i, 1])[k]
        s = 4 + 4 * i + k
        return copy(src, dst, rs_send.at[h, s], rs_recv.at[h, s], peer(h, True, 1 if k % 2 == 0 else -1))

    def reduce2(h, k):
        a, b = first[h], second[h]
        src = (
            parts.at[h, ring(a + 2), b, 0],
            parts.at[h, ring(a + 2), b, 1],
            parts.at[h, ring(a + 1), b],
            parts.at[h, ring(a - 1), b],
        )[k]
        dst = (relay2.at[h, 0], relay2.at[h, 1], full2.at[h, 0], full2.at[h, 1])[k]
        return copy(src, dst, rs_send.at[h, k], rs_recv.at[h, k], peer(h, False, 1 if k % 2 == 0 else -1))

    def start_first(i):
        for h in (0, 1):
            reduce1(h, i, 0).start()
            reduce1(h, i, 1).start()

    def relay_first(i):
        for h in (0, 1):
            g = ring(first[h] - i)
            up, down = ring(second[h] + 1), ring(second[h] - 1)
            reduce1(h, i, 0).wait_recv()
            parts[h, g, up, 0] = (parts[h, g, up, 0].astype(F32) + relay1[h, i, 0].astype(F32)).astype(BF)
            reduce1(h, i, 1).wait_recv()
            parts[h, g, down, 1] = (parts[h, g, down, 1].astype(F32) + relay1[h, i, 1].astype(F32)).astype(BF)
        for h in (0, 1):
            reduce1(h, i, 2).start()
            reduce1(h, i, 3).start()

    def collect(h, i, part, more=None):
        g, b = ring(first[h] - i), second[h]
        total = parts[h, g, b, part].astype(F32) + full1[h, i, 0, part].astype(F32) + full1[h, i, 1, part].astype(F32)
        if more is not None:
            total = total + more.astype(F32)
        return total

    def wait_first(i):
        for h in (0, 1):
            reduce1(h, i, 2).wait_recv()
            reduce1(h, i, 3).wait_recv()

    def out_copy(step):
        to = (e + step) % experts
        return copy(sendx.at[to], recvx.at[e], x_send.at[0, step], x_recv.at[0, step], (to, f))

    def out_arrival(step):
        src = (e + experts - step) % experts
        return copy(sendx.at[src], recvx.at[src], x_send.at[0, step], x_recv.at[0, step], (src, f))

    def back_copy(step):
        to = (e + step) % experts
        return copy(sendx.at[to], backx.at[e], x_send.at[1, step], x_recv.at[1, step], (to, f))

    def back_arrival(step):
        src = (e + experts - step) % experts
        return copy(sendx.at[src], backx.at[src], x_send.at[1, step], x_recv.at[1, step], (src, f))

    loads = []
    for h in (0, 1):
        for k, w in ((0, w_in), (1, w_out)):
            loads.append(
                pltpu.make_async_copy(
                    w.at[pl.ds(h * half, half)], wts.at[h, first[h], second[h], k], load_sem.at[2 * h + k]
                )
            )
    for c in loads:
        c.start()
    barrier = pltpu.get_barrier_semaphore()
    for step in range(1, experts):
        pl.semaphore_signal(barrier, inc=1, device_id=((e + step) % experts, f), device_id_type=MESH)
    for h in (0, 1):
        for step in (1, -1):
            pl.semaphore_signal(barrier, inc=1, device_id=peer(h, False, step), device_id_type=MESH)
    for c in loads:
        c.wait()
    pl.semaphore_wait(barrier, experts + 3)

    for h in (0, 1):
        gather(h, None, 0).start()
        gather(h, None, 1).start()
    for h in (0, 1):
        gather(h, 0, 0).start()
        gather(h, 0, 1).start()

    lane = lax.broadcasted_iota(jnp.int32, (16, rows), 0)
    named = [(lane == ids_row[k : k + 1, :]).astype(F32) for k in (0, 1)]
    before = (
        lax.broadcasted_iota(jnp.int32, (rows, rows), 0) < lax.broadcasted_iota(jnp.int32, (rows, rows), 1)
    ).astype(BF)
    ahead = dot((named[0] + named[1]).astype(BF), before, ((1,), (0,)))
    slot = [
        ids_row[k : k + 1, :].astype(F32) * cap + jnp.sum(named[k] * ahead, axis=0, keepdims=True) for k in (0, 1)
    ]

    def chosen(k, start, count):
        at = lax.broadcasted_iota(jnp.int32, (count, rows), 0) + start
        return (at.astype(F32) == slot[k]).astype(F32)

    def fill(d, carry):
        pick = [chosen(k, d * cap, cap) for k in (0, 1)]
        either = (pick[0] + pick[1]).astype(BF)
        gate = jnp.sum(pick[0] * gates_row[0:1, :] + pick[1] * gates_row[1:2, :], axis=1, keepdims=True)
        sendx[d, 0] = dot(either, tokens[...], ((1,), (0,))).astype(BF)
        sendx[d, 1] = (dot(either, grad_y[...], ((1,), (0,))) * gate).astype(BF)
        return carry

    lax.fori_loop(0, experts, fill, 0)
    for step in range(1, experts):
        out_copy(step).start()
    recvx[e] = sendx[e]

    for h in (0, 1):
        got(h, None, 0)
        gather(h, None, 2).start()
        gather(h, 1, 0).start()
        gather(h, 1, 1).start()
        got(h, None, 1)
        gather(h, None, 3).start()
    for h in (0, 1):
        got(h, 0, 0)
        gather(h, 0, 2).start()
        got(h, 0, 1)
        gather(h, 0, 3).start()
    for h in (0, 1):
        got(h, None, 2)
        got(h, None, 3)
        gather(h, 2, 0).start()
        gather(h, 2, 1).start()
    for h in (0, 1):
        got(h, 1, 0)
        gather(h, 1, 2).start()
        got(h, 1, 1)
        gather(h, 1, 3).start()
    for h in (0, 1):
        gather(h, 3, 0).start()
        gather(h, 3, 1).start()
    for step in range(1, experts):
        out_arrival(step).wait_recv()
    for h in (0, 1):
        got(h, 0, 2)
        got(h, 0, 3)
    acc[...] = jnp.zeros_like(acc)

    def compute(it, carry):
        i, h = it // 2, it % 2

        @pl.when(it == 2)
        def _():
            for hh in (0, 1):
                got(hh, 2, 0)
                gather(hh, 2, 2).start()
                got(hh, 2, 1)
                gather(hh, 2, 3).start()
            for hh in (0, 1):
                got(hh, 1, 2)
                got(hh, 1, 3)

        @pl.when(it == 4)
        def _():
            for hh in (0, 1):
                got(hh, 3, 0)
                gather(hh, 3, 2).start()
                got(hh, 3, 1)
                gather(hh, 3, 3).start()
            start_first(1)
            start_first(0)
            for hh in (0, 1):
                got(hh, 2, 2)
                got(hh, 2, 3)

        @pl.when(it == 6)
        def _():
            start_first(2)
            relay_first(1)
            for hh in (0, 1):
                got(hh, 3, 2)
                got(hh, 3, 3)

        g = ring(y + h * (z - y) - i)

        def weight(k, *at):
            return wts[(h, g, slice(None), k, slice(None)) + at].reshape(group, -1)

        def patches(k, *at):
            return recvx[(slice(None), k, slice(None)) + at].reshape(slots, -1)

        pre = dot(patches(0), weight(0), ((1,), (1,)))
        grad_act = dot(patches(1), weight(1), ((1,), (1,)))
        cdf = 0.5 * (1.0 + lax.erf(pre * inv_sqrt_two))
        act = pre * cdf
        hidden = grad_act * (cdf + pre * jnp.exp(-0.5 * pre * pre) * inv_sqrt_two_pi)
        act_s[...] = act.astype(BF)
        gh_s[...] = hidden.astype(BF)
        act_t[...] = act.T.astype(BF)
        gh_t[...] = hidden.T.astype(BF)

        def columns(c, inner):
            at = pl.ds(pl.multiple_of(c * tile, tile), tile)
            acc[0, :, at] += dot(act_s[...], weight(1, at), ((1,), (0,)))
            acc[1, :, at] += dot(gh_s[...], weight(0, at), ((1,), (0,)))
            parts[h, g, :, 0, :, at] = dot(gh_t[...], patches(0, at), ((1,), (0,))).astype(BF).reshape(SIDE, half, tile)
            parts[h, g, :, 1, :, at] = dot(act_t[...], patches(1, at), ((1,), (0,))).astype(BF).reshape(SIDE, half, tile)
            return inner

        lax.fori_loop(0, 3, columns, 0)
        return carry

    lax.fori_loop(0, 8, compute, 0)

    start_first(3)
    for step in range(1, experts):
        out_copy(step).wait_send()
    for d in range(experts):
        for k in (0, 1):
            sendx[d, k] = acc[k, d * cap : (d + 1) * cap, :].astype(BF)
    relay_first(2)
    for step in range(1, experts):
        back_copy(step).start()
    backx[e] = sendx[e]

    relay_first(3)
    wait_first(2)
    for h in (0, 1):
        for part in (0, 1):
            parts[h, ring(first[h] + 2), second[h], part] = collect(h, 2, part).astype(BF)
    relay_first(0)
    for h in (0, 1):
        reduce2(h, 0).start()
        reduce2(h, 1).start()
    wait_first(1)
    wait_first(3)
    for h in (0, 1):
        reduce2(h, 0).wait_recv()
        reduce2(h, 1).wait_recv()
        up, down, b = ring(first[h] + 1), ring(first[h] - 1), second[h]
        parts[h, up, b, 0] = collect(h, 3, 0, relay2[h, 0]).astype(BF)
        parts[h, up, b, 1] = collect(h, 3, 1).astype(BF)
        parts[h, down, b, 0] = collect(h, 1, 0).astype(BF)
        parts[h, down, b, 1] = collect(h, 1, 1, relay2[h, 1]).astype(BF)
    for h in (0, 1):
        reduce2(h, 2).start()
        reduce2(h, 3).start()

    for step in range(1, experts):
        back_arrival(step).wait_recv()
    pick = [chosen(k, 0, slots).astype(BF) for k in (0, 1)]
    both = pick[0] + pick[1]
    by_gate = [jnp.zeros((rows, 1), F32) for _ in (0, 1)]
    for c in range(3):
        at = slice(c * tile, (c + 1) * tile)
        results = backx[:, 0, :, at].reshape(slots, tile)
        grads = backx[:, 1, :, at].reshape(slots, tile)
        cot = grad_y[:, at].astype(F32)
        total = jnp.zeros((rows, tile), F32)
        for k in (0, 1):
            one = dot(pick[k], results, ((0,), (0,)))
            total = total + gates_col[:, k : k + 1] * one
            by_gate[k] = by_gate[k] + jnp.sum(cot * one, axis=1, keepdims=True)
        mixed[:, at] = total.astype(BF)
        grad_tokens[:, at] = dot(both, grads, ((0,), (0,))).astype(BF)
    for k in (0, 1):
        grad_gates[:, k : k + 1] = by_gate[k]

    wait_first(0)
    for h in (0, 1):
        reduce2(h, 2).wait_recv()
        reduce2(h, 3).wait_recv()
        for part, out in ((0, grad_in), (1, grad_out)):
            total = collect(h, 0, part) + full2[h, 0, part].astype(F32) + full2[h, 1, part].astype(F32)
            out[h * half : (h + 1) * half, :] = total

    for step in range(1, experts):
        back_copy(step).wait_send()
    for h in (0, 1):
        for k in range(4):
            gather(h, None, k).wait_send()
            reduce2(h, k).wait_send()
            for i in range(SIDE):
                gather(h, i, k).wait_send()
                reduce1(h, i, k).wait_send()


def shards(tokens, expert_ids, gates, w_in, w_out, grad_y):
    rows, features = tokens.shape
    experts = lax.axis_size("exp")
    cap = 3 * rows // 8
    hidden = w_in.shape[1]
    half = hidden // 2
    group = SIDE * half
    slots = experts * cap
    vmem = pl.BlockSpec(memory_space=pltpu.VMEM)
    hbm = pl.BlockSpec(memory_space=pl.ANY)
    mixed, grad_tokens, grad_in, grad_out, grad_gates = pl.pallas_call(
        functools.partial(kernel, experts),
        name="moe",
        out_shape=(
            jax.ShapeDtypeStruct((rows, features), BF),
            jax.ShapeDtypeStruct((rows, features), BF),
            jax.ShapeDtypeStruct((hidden, features), F32),
            jax.ShapeDtypeStruct((hidden, features), F32),
            jax.ShapeDtypeStruct((rows, 2), F32),
        ),
        in_specs=[vmem] * 5 + [hbm] * 2,
        out_specs=(vmem,) * 5,
        scratch_shapes=[
            pltpu.VMEM((2, SIDE, SIDE, 2, half, features), BF),
            pltpu.VMEM((2, SIDE, SIDE, 2, half, features), BF),
            pltpu.VMEM((2, SIDE, 2, half, features), BF),
            pltpu.VMEM((2, SIDE, 2, 2, half, features), BF),
            pltpu.VMEM((2, 2, half, features), BF),
            pltpu.VMEM((2, 2, 2, half, features), BF),
            pltpu.VMEM((experts, 2, cap, features), BF),
            pltpu.VMEM((experts, 2, cap, features), BF),
            pltpu.VMEM((experts, 2, cap, features), BF),
            pltpu.VMEM((2, slots, features), F32),
            pltpu.VMEM((slots, group), BF),
            pltpu.VMEM((slots, group), BF),
            pltpu.VMEM((group, slots), BF),
            pltpu.VMEM((group, slots), BF),
            pltpu.SemaphoreType.DMA((4,)),
            pltpu.SemaphoreType.DMA((2, 20)),
            pltpu.SemaphoreType.DMA((2, 20)),
            pltpu.SemaphoreType.DMA((2, 20)),
            pltpu.SemaphoreType.DMA((2, 20)),
            pltpu.SemaphoreType.DMA((2, experts)),
            pltpu.SemaphoreType.DMA((2, experts)),
        ],
        compiler_params=pltpu.CompilerParams(
            collective_id=0, has_side_effects=True, vmem_limit_bytes=66_000_000
        ),
    )(expert_ids.T, gates.T, gates, tokens, grad_y, w_in[0], w_out[0])
    return mixed, grad_tokens, grad_in[None], grad_out[None], grad_gates


def solution(mesh):
    return jax.shard_map(
        shards,
        mesh=mesh,
        in_specs=(
            P(("exp", "fsdp"), None),
            P(("exp", "fsdp"), None),
            P(("exp", "fsdp"), None),
            P("exp", "fsdp", None),
            P("exp", "fsdp", None),
            P(("exp", "fsdp"), None),
        ),
        out_specs=(
            P(("exp", "fsdp"), None),
            P(("exp", "fsdp"), None),
            P("exp", "fsdp", None),
            P("exp", "fsdp", None),
            P(("exp", "fsdp"), None),
        ),
        check_vma=False,
    )
```

```python
import functools

import jax
import jax.numpy as jnp
from jax import lax
from jax.experimental import pallas as pl
from jax.experimental.pallas import tpu as pltpu
from jax.sharding import PartitionSpec as P

inv_sqrt_two = 0.7071067811865476
inv_sqrt_two_pi = 0.3989422804014327
MESH = pl.DeviceIdType.MESH
SIDE = 4
BF = jnp.bfloat16
F32 = jnp.float32


def dot(left, right, over):
    return lax.dot_general(left, right, (over, ((), ())), preferred_element_type=F32)


def kernel(
    experts,
    ids_row,
    gates_row,
    tokens,
    grad_y,
    w_in,
    w_out,
    mixed,
    grad_tokens,
    grad_in,
    grad_out,
    grad_gates,
    wts,
    parts,
    relay1,
    full1,
    relay2,
    full2,
    sendx,
    recvx,
    backx,
    acc,
    act_s,
    gh_s,
    act_t,
    gh_t,
    load_sem,
    ag_send,
    ag_recv,
    rs_send,
    rs_recv,
    x_send,
    x_recv,
):
    rows, features = tokens.shape
    half = w_in.shape[0] // 2
    cap = sendx.shape[2]
    slots = experts * cap
    group = SIDE * half
    tile = features // 3

    e = lax.axis_index("exp")
    f = lax.axis_index("fsdp")
    z, y = f // SIDE, f % SIDE

    def ring(value):
        return (value + SIDE) % SIDE

    first, second = (y, z), (z, y)

    def peer(h, second_axis, step):
        along_z = (h == 0) == second_axis
        nz = ring(z + step) if along_z else z
        ny = y if along_z else ring(y + step)
        return (e, nz * SIDE + ny)

    def copy(src, dst, send, recv, to):
        return pltpu.make_async_remote_copy(
            src_ref=src, dst_ref=dst, send_sem=send, recv_sem=recv, device_id=to, device_id_type=MESH
        )

    def gather_region(h, i, k, sent):
        a, b = first[h], second[h]
        if i is None:
            if sent:
                return (wts.at[h, a, b], wts.at[h, a, b], wts.at[h, ring(a - 1), b, 0], wts.at[h, ring(a + 1), b, 1])[k]
            return (
                wts.at[h, ring(a - 1), b],
                wts.at[h, ring(a + 1), b],
                wts.at[h, ring(a + 2), b, 0],
                wts.at[h, ring(a + 2), b, 1],
            )[k]
        g = ring(a - i)
        if sent:
            return (wts.at[h, g, b], wts.at[h, g, b], wts.at[h, g, ring(b - 1), 0], wts.at[h, g, ring(b + 1), 1])[k]
        return (
            wts.at[h, g, ring(b - 1)],
            wts.at[h, g, ring(b + 1)],
            wts.at[h, g, ring(b + 2), 0],
            wts.at[h, g, ring(b + 2), 1],
        )[k]

    def gather(h, i, k, sent=True):
        region = gather_region(h, i, k, sent)
        s = k if i is None else 4 + 4 * i + k
        step = 1 if k % 2 == 0 else -1
        return copy(region, region, ag_send.at[h, s], ag_recv.at[h, s], peer(h, i is not None, step))

    def got(h, i, k):
        gather(h, i, k, sent=False).wait_recv()

    def reduce1(h, i, k):
        a, b = first[h], second[h]
        g = ring(a - i)
        src = (
            parts.at[h, g, ring(b + 2), 0],
            parts.at[h, g, ring(b + 2), 1],
            parts.at[h, g, ring(b + 1)],
            parts.at[h, g, ring(b - 1)],
        )[k]
        dst = (relay1.at[h, i, 0], relay1.at[h, i, 1], full1.at[h, i, 0], full1.at[h, i, 1])[k]
        s = 4 + 4 * i + k
        return copy(src, dst, rs_send.at[h, s], rs_recv.at[h, s], peer(h, True, 1 if k % 2 == 0 else -1))

    def reduce2(h, k):
        a, b = first[h], second[h]
        src = (
            parts.at[h, ring(a + 2), b, 0],
            parts.at[h, ring(a + 2), b, 1],
            parts.at[h, ring(a + 1), b],
            parts.at[h, ring(a - 1), b],
        )[k]
        dst = (relay2.at[h, 0], relay2.at[h, 1], full2.at[h, 0], full2.at[h, 1])[k]
        return copy(src, dst, rs_send.at[h, k], rs_recv.at[h, k], peer(h, False, 1 if k % 2 == 0 else -1))

    def start_first(i):
        for h in (0, 1):
            reduce1(h, i, 0).start()
            reduce1(h, i, 1).start()

    def relay_first(i):
        for h in (0, 1):
            g = ring(first[h] - i)
            up, down = ring(second[h] + 1), ring(second[h] - 1)
            reduce1(h, i, 0).wait_recv()
            parts[h, g, up, 0] = (parts[h, g, up, 0].astype(F32) + relay1[h, i, 0].astype(F32)).astype(BF)
            reduce1(h, i, 1).wait_recv()
            parts[h, g, down, 1] = (parts[h, g, down, 1].astype(F32) + relay1[h, i, 1].astype(F32)).astype(BF)
        for h in (0, 1):
            reduce1(h, i, 2).start()
            reduce1(h, i, 3).start()

    def collect(h, i, part, more=None):
        g, b = ring(first[h] - i), second[h]
        total = parts[h, g, b, part].astype(F32) + full1[h, i, 0, part].astype(F32) + full1[h, i, 1, part].astype(F32)
        if more is not None:
            total = total + more.astype(F32)
        return total

    def wait_first(i):
        for h in (0, 1):
            reduce1(h, i, 2).wait_recv()
            reduce1(h, i, 3).wait_recv()

    def out_copy(step):
        to = (e + step) % experts
        return copy(sendx.at[to], recvx.at[e], x_send.at[0, step], x_recv.at[0, step], (to, f))

    def out_arrival(step):
        src = (e + experts - step) % experts
        return copy(sendx.at[src], recvx.at[src], x_send.at[0, step], x_recv.at[0, step], (src, f))

    def back_copy(step):
        to = (e + step) % experts
        return copy(sendx.at[to], backx.at[e], x_send.at[1, step], x_recv.at[1, step], (to, f))

    def back_arrival(step):
        src = (e + experts - step) % experts
        return copy(sendx.at[src], backx.at[src], x_send.at[1, step], x_recv.at[1, step], (src, f))

    loads = []
    for h in (0, 1):
        for k, w in ((0, w_in), (1, w_out)):
            loads.append(
                pltpu.make_async_copy(
                    w.at[pl.ds(h * half, half)], wts.at[h, first[h], second[h], k], load_sem.at[2 * h + k]
                )
            )
    for c in loads:
        c.start()
    barrier = pltpu.get_barrier_semaphore()
    for step in range(1, experts):
        pl.semaphore_signal(barrier, inc=1, device_id=((e + step) % experts, f), device_id_type=MESH)
    for h in (0, 1):
        for step in (1, -1):
            pl.semaphore_signal(barrier, inc=1, device_id=peer(h, False, step), device_id_type=MESH)
    for c in loads:
        c.wait()
    pl.semaphore_wait(barrier, experts + 3)

    for h in (0, 1):
        gather(h, None, 0).start()
        gather(h, None, 1).start()
    for h in (0, 1):
        gather(h, 0, 0).start()
        gather(h, 0, 1).start()

    lane = lax.broadcasted_iota(jnp.int32, (16, rows), 0)
    named = [(lane == ids_row[k : k + 1, :]).astype(F32) for k in (0, 1)]
    before = (
        lax.broadcasted_iota(jnp.int32, (rows, rows), 0) < lax.broadcasted_iota(jnp.int32, (rows, rows), 1)
    ).astype(BF)
    ahead = dot((named[0] + named[1]).astype(BF), before, ((1,), (0,)))
    slot = [
        ids_row[k : k + 1, :].astype(F32) * cap + jnp.sum(named[k] * ahead, axis=0, keepdims=True) for k in (0, 1)
    ]

    def chosen(k, start, count):
        at = lax.broadcasted_iota(jnp.int32, (count, rows), 0) + start
        return (at.astype(F32) == slot[k]).astype(F32)

    def fill(d, carry):
        pick = [chosen(k, d * cap, cap) for k in (0, 1)]
        either = (pick[0] + pick[1]).astype(BF)
        gate = jnp.sum(pick[0] * gates_row[0:1, :] + pick[1] * gates_row[1:2, :], axis=1, keepdims=True)
        sendx[d, 0] = dot(either, tokens[...], ((1,), (0,))).astype(BF)
        sendx[d, 1] = (dot(either, grad_y[...], ((1,), (0,))) * gate).astype(BF)
        return carry

    lax.fori_loop(0, experts, fill, 0)
    for step in range(1, experts):
        out_copy(step).start()
    recvx[e] = sendx[e]

    for h in (0, 1):
        got(h, None, 0)
        gather(h, None, 2).start()
        gather(h, 1, 0).start()
        gather(h, 1, 1).start()
        got(h, None, 1)
        gather(h, None, 3).start()
    for h in (0, 1):
        got(h, 0, 0)
        gather(h, 0, 2).start()
        got(h, 0, 1)
        gather(h, 0, 3).start()
    for h in (0, 1):
        got(h, None, 2)
        got(h, None, 3)
        gather(h, 2, 0).start()
        gather(h, 2, 1).start()
    for h in (0, 1):
        got(h, 1, 0)
        gather(h, 1, 2).start()
        got(h, 1, 1)
        gather(h, 1, 3).start()
    for h in (0, 1):
        gather(h, 3, 0).start()
        gather(h, 3, 1).start()
    for step in range(1, experts):
        out_arrival(step).wait_recv()
    for h in (0, 1):
        got(h, 0, 2)
        got(h, 0, 3)
    acc[...] = jnp.zeros_like(acc)

    def compute(it, carry):
        i, h = it // 2, it % 2

        @pl.when(it == 2)
        def _():
            for hh in (0, 1):
                got(hh, 2, 0)
                gather(hh, 2, 2).start()
                got(hh, 2, 1)
                gather(hh, 2, 3).start()
            for hh in (0, 1):
                got(hh, 1, 2)
                got(hh, 1, 3)

        @pl.when(it == 4)
        def _():
            for hh in (0, 1):
                got(hh, 3, 0)
                gather(hh, 3, 2).start()
                got(hh, 3, 1)
                gather(hh, 3, 3).start()
            start_first(1)
            start_first(0)
            for hh in (0, 1):
                got(hh, 2, 2)
                got(hh, 2, 3)

        @pl.when(it == 6)
        def _():
            start_first(2)
            relay_first(1)
            for hh in (0, 1):
                got(hh, 3, 2)
                got(hh, 3, 3)

        g = ring(y + h * (z - y) - i)

        def weight(k, *at):
            return wts[(h, g, slice(None), k, slice(None)) + at].reshape(group, -1)

        def patches(k, *at):
            return recvx[(slice(None), k, slice(None)) + at].reshape(slots, -1)

        pre = dot(patches(0), weight(0), ((1,), (1,)))
        grad_act = dot(patches(1), weight(1), ((1,), (1,)))
        cdf = 0.5 * (1.0 + lax.erf(pre * inv_sqrt_two))
        act = pre * cdf
        hidden = grad_act * (cdf + pre * jnp.exp(-0.5 * pre * pre) * inv_sqrt_two_pi)
        act_s[...] = act.astype(BF)
        gh_s[...] = hidden.astype(BF)
        act_t[...] = act.T.astype(BF)
        gh_t[...] = hidden.T.astype(BF)

        def columns(c, inner):
            at = pl.ds(pl.multiple_of(c * tile, tile), tile)
            acc[0, :, at] += dot(act_s[...], weight(1, at), ((1,), (0,)))
            acc[1, :, at] += dot(gh_s[...], weight(0, at), ((1,), (0,)))
            parts[h, g, :, 0, :, at] = dot(gh_t[...], patches(0, at), ((1,), (0,))).astype(BF).reshape(SIDE, half, tile)
            parts[h, g, :, 1, :, at] = dot(act_t[...], patches(1, at), ((1,), (0,))).astype(BF).reshape(SIDE, half, tile)
            return inner

        lax.fori_loop(0, 3, columns, 0)
        return carry

    lax.fori_loop(0, 8, compute, 0)

    start_first(3)
    for step in range(1, experts):
        out_copy(step).wait_send()
    for d in range(experts):
        for k in (0, 1):
            sendx[d, k] = acc[k, d * cap : (d + 1) * cap, :].astype(BF)
    relay_first(2)
    for step in range(1, experts):
        back_copy(step).start()
    backx[e] = sendx[e]

    relay_first(3)
    wait_first(2)
    for h in (0, 1):
        for part in (0, 1):
            parts[h, ring(first[h] + 2), second[h], part] = collect(h, 2, part).astype(BF)
    relay_first(0)
    for h in (0, 1):
        reduce2(h, 0).start()
        reduce2(h, 1).start()
    wait_first(1)
    wait_first(3)
    for h in (0, 1):
        reduce2(h, 0).wait_recv()
        reduce2(h, 1).wait_recv()
        up, down, b = ring(first[h] + 1), ring(first[h] - 1), second[h]
        parts[h, up, b, 0] = collect(h, 3, 0, relay2[h, 0]).astype(BF)
        parts[h, up, b, 1] = collect(h, 3, 1).astype(BF)
        parts[h, down, b, 0] = collect(h, 1, 0).astype(BF)
        parts[h, down, b, 1] = collect(h, 1, 1, relay2[h, 1]).astype(BF)
    for h in (0, 1):
        reduce2(h, 2).start()
        reduce2(h, 3).start()

    for step in range(1, experts):
        back_arrival(step).wait_recv()
    pick = [chosen(k, 0, slots).astype(BF) for k in (0, 1)]
    both = pick[0] + pick[1]
    square = (rows, rows)
    diagonal = (
        lax.broadcasted_iota(jnp.int32, square, 0) == lax.broadcasted_iota(jnp.int32, square, 1)
    ).astype(F32)
    gate_col = [jnp.sum(diagonal * gates_row[k : k + 1, :], axis=1, keepdims=True) for k in (0, 1)]
    by_gate = [jnp.zeros((rows, 1), F32) for _ in (0, 1)]
    for c in range(3):
        at = slice(c * tile, (c + 1) * tile)
        results = backx[:, 0, :, at].reshape(slots, tile)
        grads = backx[:, 1, :, at].reshape(slots, tile)
        cot = grad_y[:, at].astype(F32)
        total = jnp.zeros((rows, tile), F32)
        for k in (0, 1):
            one = dot(pick[k], results, ((0,), (0,)))
            total = total + gate_col[k] * one
            by_gate[k] = by_gate[k] + jnp.sum(cot * one, axis=1, keepdims=True)
        mixed[:, at] = total.astype(BF)
        grad_tokens[:, at] = dot(both, grads, ((0,), (0,))).astype(BF)
    for k in (0, 1):
        grad_gates[k : k + 1, :] = jnp.sum(diagonal * by_gate[k], axis=0, keepdims=True)

    wait_first(0)
    for h in (0, 1):
        reduce2(h, 2).wait_recv()
        reduce2(h, 3).wait_recv()
        for part, out in ((0, grad_in), (1, grad_out)):
            total = collect(h, 0, part) + full2[h, 0, part].astype(F32) + full2[h, 1, part].astype(F32)
            out[h * half : (h + 1) * half, :] = total

    for step in range(1, experts):
        back_copy(step).wait_send()
    for h in (0, 1):
        for k in range(4):
            gather(h, None, k).wait_send()
            reduce2(h, k).wait_send()
            for i in range(SIDE):
                gather(h, i, k).wait_send()
                reduce1(h, i, k).wait_send()


def place(*refs):
    given, taken, held, (into, outof) = refs[:5], refs[5:10], refs[10:15], refs[15:]
    ins = [pltpu.make_async_copy(given[k], held[k], into.at[k]) for k in range(5)]
    outs = [pltpu.make_async_copy(held[k], taken[k], outof.at[k]) for k in range(5)]
    for c in ins:
        c.start()
    for k in range(5):
        ins[k].wait()
        outs[k].start()
    for c in outs:
        c.wait()


def shards(tokens, expert_ids, gates, w_in, w_out, grad_y):
    rows, features = tokens.shape
    experts = lax.axis_size("exp")
    cap = 3 * rows // 8
    hidden = w_in.shape[1]
    half = hidden // 2
    group = SIDE * half
    slots = experts * cap
    vmem = pl.BlockSpec(memory_space=pltpu.VMEM)
    hbm = pl.BlockSpec(memory_space=pl.ANY)
    mixed, grad_tokens, grad_in, grad_out, grad_gates = pl.pallas_call(
        functools.partial(kernel, experts),
        name="moe",
        out_shape=(
            jax.ShapeDtypeStruct((rows, features), BF),
            jax.ShapeDtypeStruct((rows, features), BF),
            jax.ShapeDtypeStruct((hidden, features), F32),
            jax.ShapeDtypeStruct((hidden, features), F32),
            jax.ShapeDtypeStruct((2, rows), F32),
        ),
        in_specs=[vmem] * 4 + [hbm] * 2,
        out_specs=(vmem,) * 5,
        scratch_shapes=[
            pltpu.VMEM((2, SIDE, SIDE, 2, half, features), BF),
            pltpu.VMEM((2, SIDE, SIDE, 2, half, features), BF),
            pltpu.VMEM((2, SIDE, 2, half, features), BF),
            pltpu.VMEM((2, SIDE, 2, 2, half, features), BF),
            pltpu.VMEM((2, 2, half, features), BF),
            pltpu.VMEM((2, 2, 2, half, features), BF),
            pltpu.VMEM((experts, 2, cap, features), BF),
            pltpu.VMEM((experts, 2, cap, features), BF),
            pltpu.VMEM((experts, 2, cap, features), BF),
            pltpu.VMEM((2, slots, features), F32),
            pltpu.VMEM((slots, group), BF),
            pltpu.VMEM((slots, group), BF),
            pltpu.VMEM((group, slots), BF),
            pltpu.VMEM((group, slots), BF),
            pltpu.SemaphoreType.DMA((4,)),
            pltpu.SemaphoreType.DMA((2, 20)),
            pltpu.SemaphoreType.DMA((2, 20)),
            pltpu.SemaphoreType.DMA((2, 20)),
            pltpu.SemaphoreType.DMA((2, 20)),
            pltpu.SemaphoreType.DMA((2, experts)),
            pltpu.SemaphoreType.DMA((2, experts)),
        ],
        compiler_params=pltpu.CompilerParams(
            collective_id=0, has_side_effects=True, vmem_limit_bytes=66_000_000
        ),
    )(expert_ids.T, gates.T, tokens, grad_y, w_in[0], w_out[0])
    results = (grad_in, grad_out, mixed, grad_tokens, grad_gates)
    grad_in, grad_out, mixed, grad_tokens, grad_gates = pl.pallas_call(
        place,
        name="place",
        out_shape=tuple(jax.ShapeDtypeStruct(r.shape, r.dtype) for r in results),
        in_specs=[hbm] * 5,
        out_specs=(hbm,) * 5,
        scratch_shapes=[pltpu.VMEM(r.shape, r.dtype) for r in results]
        + [pltpu.SemaphoreType.DMA((5,)), pltpu.SemaphoreType.DMA((5,))],
    )(*results)
    return mixed, grad_tokens, grad_in[None], grad_out[None], grad_gates.T


def solution(mesh):
    return jax.shard_map(
        shards,
        mesh=mesh,
        in_specs=(
            P(("exp", "fsdp"), None),
            P(("exp", "fsdp"), None),
            P(("exp", "fsdp"), None),
            P("exp", "fsdp", None),
            P("exp", "fsdp", None),
            P(("exp", "fsdp"), None),
        ),
        out_specs=(
            P(("exp", "fsdp"), None),
            P(("exp", "fsdp"), None),
            P("exp", "fsdp", None),
            P("exp", "fsdp", None),
            P(("exp", "fsdp"), None),
        ),
        check_vma=False,
    )
```

```python
import functools

import jax
import jax.numpy as jnp
from jax import lax
from jax.experimental import pallas as pl
from jax.experimental.pallas import tpu as pltpu
from jax.sharding import PartitionSpec as P

inv_sqrt_two = 0.7071067811865476
inv_sqrt_two_pi = 0.3989422804014327
MESH = pl.DeviceIdType.MESH
SIDE = 4
BF = jnp.bfloat16
F32 = jnp.float32


def dot(left, right, over):
    return lax.dot_general(left, right, (over, ((), ())), preferred_element_type=F32)


def kernel(
    experts,
    ids_row,
    gates_row,
    tokens,
    grad_y,
    w_in,
    w_out,
    mixed,
    grad_tokens,
    grad_in,
    grad_out,
    grad_gates,
    wts,
    parts0,
    parts1,
    relay0,
    full0,
    last0,
    mate1,
    relay1,
    full1,
    raw_tokens,
    raw_grads,
    raw_ids,
    raw_gates,
    sendx,
    recvx,
    backx,
    acc,
    act_s,
    gh_s,
    act_t,
    gh_t,
    load_sem,
    raw_send,
    raw_recv,
    ag_send,
    ag_recv,
    rs_send,
    rs_recv,
    x_send,
    x_recv,
):
    rows, features = tokens.shape
    half = w_in.shape[0] // 2
    cap = sendx.shape[3]
    slots = experts * cap
    group = SIDE * half
    tile = features // 3

    e = lax.axis_index("exp")
    f = lax.axis_index("fsdp")
    z, y = f // SIDE, f % SIDE
    odd = y % 2
    side = y // 2
    toward = 1 - 2 * odd

    def ring(value):
        return (value + SIDE) % SIDE

    first, second = (y, z), (z, y)

    def axis_of(h, i):
        return "yz"[(h + (i is not None)) % 2]

    def step_of(axis, k):
        if axis == "z":
            return 1 if k % 2 == 0 else -1
        return toward if k % 2 == 0 else -toward

    def peer(axis, k):
        step = step_of(axis, k)
        return (e, ring(z + step) * SIDE + y if axis == "z" else z * SIDE + ring(y + step))

    def copy(src, dst, send, recv, to):
        return pltpu.make_async_remote_copy(
            src_ref=src, dst_ref=dst, send_sem=send, recv_sem=recv, device_id=to, device_id_type=MESH
        )

    def held(h, i):
        return ring(y + toward * i) if h == 0 else ring(z - i)

    def weights(h, i, offset, part=None):
        if i is None:
            at = (h, ring(first[h] + offset), second[h])
        else:
            at = (h, held(h, i), ring(second[h] + offset))
        return wts.at[at if part is None else at + (part,)]

    def gather(h, i, k):
        axis = axis_of(h, i)
        region = weights(h, i, 0) if k < 2 else weights(h, i, -step_of(axis, k), k - 2)
        s = k if i is None else 4 + 4 * i + k
        return copy(region, region, ag_send.at[h, s], ag_recv.at[h, s], peer(axis, k))

    def got(h, i, k):
        axis = axis_of(h, i)
        if k < 2:
            region = weights(h, i, -step_of(axis, k) if axis == "z" else step_of(axis, k))
        else:
            region = weights(h, i, 2, k - 2)
        s = k if i is None else 4 + 4 * i + k
        copy(region, region, ag_send.at[h, s], ag_recv.at[h, s], peer(axis, k)).wait_recv()

    def send(h, i):
        gather(h, i, 0).start()
        gather(h, i, 1).start()

    def forward(h, i, k):
        got(h, i, k - 2 if axis_of(h, i) == "z" else 3 - k)
        gather(h, i, k).start()

    def whole(h, i):
        got(h, i, 2)
        got(h, i, 3)

    raws = [
        copy(src, dst, raw_send.at[k], raw_recv.at[k], peer("y", 1))
        for k, (src, dst) in enumerate(
            ((ids_row, raw_ids), (gates_row, raw_gates), (tokens, raw_tokens), (grad_y, raw_grads))
        )
    ]

    def out_copy(line, step):
        to = (e + step) % experts
        return copy(sendx.at[line, to], recvx.at[line, e], x_send.at[line, step], x_recv.at[line, step], (to, f))

    def out_arrival(line, step):
        src = (e + experts - step) % experts
        return copy(sendx.at[line, src], recvx.at[line, src], x_send.at[line, step], x_recv.at[line, step], (src, f))

    def back_copy(step):
        to = (e + step) % experts
        return copy(sendx.at[0, to], backx.at[e], x_send.at[2, step], x_recv.at[2, step], (to, f))

    def back_arrival(step):
        src = (e + experts - step) % experts
        return copy(sendx.at[0, src], backx.at[src], x_send.at[2, step], x_recv.at[2, step], (src, f))

    def ring0(j, k):
        src = (
            parts0.at[j, ring(z + 2), 0],
            parts0.at[j, ring(z + 2), 1],
            parts0.at[j, ring(z + 1)],
            parts0.at[j, ring(z - 1)],
        )[k]
        dst = (relay0.at[j, 0], relay0.at[j, 1], full0.at[j, 0], full0.at[j, 1])[k]
        return copy(src, dst, rs_send.at[0, 4 * j + k], rs_recv.at[0, 4 * j + k], peer("z", k))

    def mate0():
        return copy(parts0.at[1, z], last0, rs_send.at[0, 8], rs_recv.at[0, 8], peer("y", 0))

    def to_mate1(i):
        return copy(parts1.at[i, 1 - odd], mate1.at[i], rs_send.at[1, i], rs_recv.at[1, i], peer("y", 0))

    def ring1(k):
        src = (parts1.at[2, odd, 0], parts1.at[2, odd, 1], parts1.at[3, odd], parts1.at[1, odd])[k]
        dst = (relay1.at[0], relay1.at[1], full1.at[0], full1.at[1])[k]
        return copy(src, dst, rs_send.at[1, 4 + k], rs_recv.at[1, 4 + k], peer("z", k))

    def add(*terms):
        total = terms[0].astype(F32)
        for t in terms[1:]:
            total = total + t.astype(F32)
        return total

    def relay_ring0(j):
        up, down = ring(z + 1), ring(z - 1)
        ring0(j, 0).wait_recv()
        parts0[j, up, 0] = add(parts0[j, up, 0], relay0[j, 0]).astype(BF)
        ring0(j, 1).wait_recv()
        parts0[j, down, 1] = add(parts0[j, down, 1], relay0[j, 1]).astype(BF)
        ring0(j, 2).start()
        ring0(j, 3).start()

    loads = []
    for h in (0, 1):
        for k, w in ((0, w_in), (1, w_out)):
            loads.append(
                pltpu.make_async_copy(
                    w.at[pl.ds(h * half, half)], wts.at[h, first[h], second[h], k], load_sem.at[2 * h + k]
                )
            )
    for c in loads:
        c.start()
    barrier = pltpu.get_barrier_semaphore()
    for step in range(1, experts):
        pl.semaphore_signal(barrier, inc=1, device_id=((e + step) % experts, f), device_id_type=MESH)
    for axis in "yz":
        for k in (0, 1):
            pl.semaphore_signal(barrier, inc=1, device_id=peer(axis, k), device_id_type=MESH)
    for c in loads:
        c.wait()
    pl.semaphore_wait(barrier, experts + 3)

    send(0, None)
    for c in raws:
        c.start()
    send(1, None)
    send(0, 0)
    send(1, 0)

    def slots_of(ids):
        lane = lax.broadcasted_iota(jnp.int32, (16, rows), 0)
        named = [(lane == ids[k : k + 1, :]).astype(F32) for k in (0, 1)]
        before = (
            lax.broadcasted_iota(jnp.int32, (rows, rows), 0) < lax.broadcasted_iota(jnp.int32, (rows, rows), 1)
        ).astype(BF)
        ahead = dot((named[0] + named[1]).astype(BF), before, ((1,), (0,)))
        return [
            ids[k : k + 1, :].astype(F32) * cap + jnp.sum(named[k] * ahead, axis=0, keepdims=True) for k in (0, 1)
        ]

    def chosen(slot, start, count):
        at = lax.broadcasted_iota(jnp.int32, (count, rows), 0) + start
        return (at.astype(F32) == slot).astype(F32)

    def dispatch(line, ids, gates, patch, cotangent):
        slot = slots_of(ids)

        def fill(d, carry):
            pick = [chosen(slot[k], d * cap, cap) for k in (0, 1)]
            either = (pick[0] + pick[1]).astype(BF)
            gate = jnp.sum(pick[0] * gates[0:1, :] + pick[1] * gates[1:2, :], axis=1, keepdims=True)
            sendx[line, d, 0] = dot(either, patch[...], ((1,), (0,))).astype(BF)
            sendx[line, d, 1] = (dot(either, cotangent[...], ((1,), (0,))) * gate).astype(BF)
            return carry

        lax.fori_loop(0, experts, fill, 0)
        for step in range(1, experts):
            out_copy(line, step).start()
        recvx[line, e] = sendx[line, e]

    dispatch(0, ids_row, gates_row, tokens, grad_y)

    forward(0, None, 3)
    send(0, 1)
    forward(0, None, 2)
    send(0, 3)
    forward(1, None, 2)
    send(1, 1)
    forward(1, None, 3)
    send(1, 3)
    forward(0, 0, 2)
    forward(0, 0, 3)
    forward(1, 0, 3)
    whole(1, None)
    send(1, 2)
    for c in raws:
        c.wait_recv()
    dispatch(1, raw_ids, raw_gates, raw_tokens, raw_grads)
    forward(0, 1, 2)
    forward(0, 1, 3)
    whole(0, None)
    send(0, 2)
    forward(0, 3, 2)
    forward(0, 3, 3)
    acc[...] = jnp.zeros_like(acc)
    for step in range(1, experts):
        out_arrival(0, step).wait_recv()

    def gelu(pre):
        cdf = 0.5 * (1.0 + lax.erf(pre * inv_sqrt_two))
        return pre * cdf, cdf + pre * jnp.exp(-0.5 * pre * pre) * inv_sqrt_two_pi

    def results(h, i):
        g = (1 - h) * ring(y + toward * i) + h * ring(z - i)

        def weight(k, *at):
            return wts[(h, g, slice(None), k, slice(None)) + at].reshape(group, -1)

        def patches(k):
            return recvx[0, :, k].reshape(slots, features)

        act, slope = gelu(dot(patches(0), weight(0), ((1,), (1,))))
        act_s[...] = act.astype(BF)
        gh_s[...] = (dot(patches(1), weight(1), ((1,), (1,))) * slope).astype(BF)

        def columns(c, inner):
            at = pl.ds(pl.multiple_of(c * tile, tile), tile)
            acc[0, :, at] += dot(act_s[...], weight(1, at), ((1,), (0,)))
            acc[1, :, at] += dot(gh_s[...], weight(0, at), ((1,), (0,)))
            return inner

        lax.fori_loop(0, 3, columns, 0)

    def gradients(h, q):
        def weight(k, at):
            if h == 0:
                return wts[0, held(0, q), :, k, :, at].reshape(group, -1)
            pair = [wts[1, held(1, i), pl.ds(2 * side, 2), k, :, at].reshape(group // 2, -1) for i in (q, q + 1)]
            return jnp.concatenate(pair, axis=0)

        every = slice(None)

        def line_of(line, inner):
            act, slope = gelu(dot(recvx[line, :, 0].reshape(slots, features), weight(0, every), ((1,), (1,))))
            hidden = dot(recvx[line, :, 1].reshape(slots, features), weight(1, every), ((1,), (1,))) * slope
            at = pl.ds(pl.multiple_of(line * slots, slots), slots)
            act_t[:, at] = act.T.astype(BF)
            gh_t[:, at] = hidden.T.astype(BF)
            return inner

        lax.fori_loop(0, 2, line_of, 0)

        def columns(c, inner):
            at = pl.ds(pl.multiple_of(c * tile, tile), tile)
            for k, left in ((0, gh_t), (1, act_t)):
                part = dot(left[...], recvx[:, :, k, :, at].reshape(2 * slots, tile), ((1,), (0,))).astype(BF)
                if h == 0:
                    parts0[q, :, k, :, at] = part.reshape(SIDE, half, tile)
                else:
                    parts1[pl.ds(q, 2), :, k, :, at] = part.reshape(2, 2, half, tile)
            return inner

        lax.fori_loop(0, 3, columns, 0)

    def first_results(it, power):
        @pl.when(it == 0)
        def _():
            whole(0, 0)

        @pl.when(it == 1)
        def _():
            forward(1, 0, 2)
            whole(0, 1)

        @pl.when(it == 2)
        def _():
            forward(1, 1, 3)
            forward(0, 2, 2)
            forward(0, 2, 3)
            whole(0, 3)

        results(0, (0o310 // power) % 8)
        return power * 8

    lax.fori_loop(0, 3, first_results, 1)

    forward(1, 1, 2)
    forward(1, 3, 3)
    forward(1, 2, 3)
    for step in range(1, experts):
        out_arrival(1, step).wait_recv()
    gradients(1, 2)
    to_mate1(2).start()
    to_mate1(3).start()
    forward(1, 3, 2)
    gradients(1, 0)
    to_mate1(1).start()
    to_mate1(0).start()
    gradients(0, 1)
    ring0(1, 0).start()
    ring0(1, 1).start()
    gradients(0, 0)
    ring0(0, 0).start()
    ring0(0, 1).start()
    forward(1, 2, 2)

    def last_results(it, power):
        @pl.when(it == 0)
        def _():
            whole(0, 2)
            to_mate1(2).wait_recv()
            parts1[2, odd] = add(parts1[2, odd], mate1[2]).astype(BF)

        @pl.when(it == 1)
        def _():
            ring1(0).start()
            ring1(1).start()
            relay_ring0(1)
            whole(1, 0)

        @pl.when(it == 2)
        def _():
            relay_ring0(0)
            whole(1, 1)

        @pl.when(it == 3)
        def _():
            whole(1, 3)

        @pl.when(it == 4)
        def _():
            whole(1, 2)

        results((0o11110 // power) % 8, (0o23102 // power) % 8)
        return power * 8

    lax.fori_loop(0, 5, last_results, 1)

    for step in range(1, experts):
        out_copy(0, step).wait_send()
    for d in range(experts):
        for k in (0, 1):
            sendx[0, d, k] = acc[k, d * cap : (d + 1) * cap, :].astype(BF)
    for step in range(1, experts):
        back_copy(step).start()
    backx[e] = sendx[0, e]

    to_mate1(3).wait_recv()
    to_mate1(1).wait_recv()
    ring1(0).wait_recv()
    ring1(1).wait_recv()
    parts1[3, odd, 0] = add(parts1[3, odd, 0], mate1[3, 0], relay1[0]).astype(BF)
    parts1[3, odd, 1] = add(parts1[3, odd, 1], mate1[3, 1]).astype(BF)
    parts1[1, odd, 0] = add(parts1[1, odd, 0], mate1[1, 0]).astype(BF)
    parts1[1, odd, 1] = add(parts1[1, odd, 1], mate1[1, 1], relay1[1]).astype(BF)
    ring1(2).start()
    ring1(3).start()
    ring0(1, 2).wait_recv()
    ring0(1, 3).wait_recv()
    parts0[1, z] = add(parts0[1, z], full0[1, 0], full0[1, 1]).astype(BF)
    mate0().start()

    to_mate1(0).wait_recv()
    ring1(2).wait_recv()
    ring1(3).wait_recv()
    for part, out in ((0, grad_in), (1, grad_out)):
        out[half : 2 * half, :] = add(
            parts1[0, odd, part], mate1[0, part], full1[0, part], full1[1, part]
        )
    ring0(0, 2).wait_recv()
    ring0(0, 3).wait_recv()
    mate0().wait_recv()
    for part, out in ((0, grad_in), (1, grad_out)):
        out[0:half, :] = add(parts0[0, z, part], full0[0, 0, part], full0[0, 1, part], last0[part])

    for step in range(1, experts):
        back_arrival(step).wait_recv()
    slot = slots_of(ids_row)
    pick = [chosen(slot[k], 0, slots).astype(BF) for k in (0, 1)]
    both = pick[0] + pick[1]
    square = (rows, rows)
    diagonal = (
        lax.broadcasted_iota(jnp.int32, square, 0) == lax.broadcasted_iota(jnp.int32, square, 1)
    ).astype(F32)
    gate_col = [jnp.sum(diagonal * gates_row[k : k + 1, :], axis=1, keepdims=True) for k in (0, 1)]
    by_gate = [jnp.zeros((rows, 1), F32) for _ in (0, 1)]
    for c in range(3):
        at = slice(c * tile, (c + 1) * tile)
        outs = backx[:, 0, :, at].reshape(slots, tile)
        grads = backx[:, 1, :, at].reshape(slots, tile)
        cot = grad_y[:, at].astype(F32)
        total = jnp.zeros((rows, tile), F32)
        for k in (0, 1):
            one = dot(pick[k], outs, ((0,), (0,)))
            total = total + gate_col[k] * one
            by_gate[k] = by_gate[k] + jnp.sum(cot * one, axis=1, keepdims=True)
        mixed[:, at] = total.astype(BF)
        grad_tokens[:, at] = dot(both, grads, ((0,), (0,))).astype(BF)
    for k in (0, 1):
        grad_gates[k : k + 1, :] = jnp.sum(diagonal * by_gate[k], axis=0, keepdims=True)

    for c in raws:
        c.wait_send()
    for step in range(1, experts):
        out_copy(1, step).wait_send()
        back_copy(step).wait_send()
    mate0().wait_send()
    for k in range(4):
        to_mate1(k).wait_send()
        ring1(k).wait_send()
        for j in (0, 1):
            ring0(j, k).wait_send()
        for h in (0, 1):
            for i in (None, 0, 1, 2, 3):
                gather(h, i, k).wait_send()


def place(*refs):
    given, taken, held, (into, outof) = refs[:5], refs[5:10], refs[10:15], refs[15:]
    ins = [pltpu.make_async_copy(given[k], held[k], into.at[k]) for k in range(5)]
    outs = [pltpu.make_async_copy(held[k], taken[k], outof.at[k]) for k in range(5)]
    for c in ins:
        c.start()
    for k in range(5):
        ins[k].wait()
        outs[k].start()
    for c in outs:
        c.wait()


def shards(tokens, expert_ids, gates, w_in, w_out, grad_y):
    rows, features = tokens.shape
    experts = lax.axis_size("exp")
    cap = 3 * rows // 8
    hidden = w_in.shape[1]
    half = hidden // 2
    group = SIDE * half
    slots = experts * cap
    vmem = pl.BlockSpec(memory_space=pltpu.VMEM)
    hbm = pl.BlockSpec(memory_space=pl.ANY)
    mixed, grad_tokens, grad_in, grad_out, grad_gates = pl.pallas_call(
        functools.partial(kernel, experts),
        name="moe",
        out_shape=(
            jax.ShapeDtypeStruct((rows, features), BF),
            jax.ShapeDtypeStruct((rows, features), BF),
            jax.ShapeDtypeStruct((hidden, features), F32),
            jax.ShapeDtypeStruct((hidden, features), F32),
            jax.ShapeDtypeStruct((2, rows), F32),
        ),
        in_specs=[vmem] * 4 + [hbm] * 2,
        out_specs=(vmem,) * 5,
        scratch_shapes=[
            pltpu.VMEM((2, SIDE, SIDE, 2, half, features), BF),
            pltpu.VMEM((2, SIDE, 2, half, features), BF),
            pltpu.VMEM((SIDE, 2, 2, half, features), BF),
            pltpu.VMEM((2, 2, half, features), BF),
            pltpu.VMEM((2, 2, 2, half, features), BF),
            pltpu.VMEM((2, half, features), BF),
            pltpu.VMEM((SIDE, 2, half, features), BF),
            pltpu.VMEM((2, half, features), BF),
            pltpu.VMEM((2, 2, half, features), BF),
            pltpu.VMEM((rows, features), BF),
            pltpu.VMEM((rows, features), BF),
            pltpu.VMEM((2, rows), jnp.int32),
            pltpu.VMEM((2, rows), F32),
            pltpu.VMEM((2, experts, 2, cap, features), BF),
            pltpu.VMEM((2, experts, 2, cap, features), BF),
            pltpu.VMEM((experts, 2, cap, features), BF),
            pltpu.VMEM((2, slots, features), F32),
            pltpu.VMEM((slots, group), BF),
            pltpu.VMEM((slots, group), BF),
            pltpu.VMEM((group, 2 * slots), BF),
            pltpu.VMEM((group, 2 * slots), BF),
            pltpu.SemaphoreType.DMA((4,)),
            pltpu.SemaphoreType.DMA((4,)),
            pltpu.SemaphoreType.DMA((4,)),
            pltpu.SemaphoreType.DMA((2, 20)),
            pltpu.SemaphoreType.DMA((2, 20)),
            pltpu.SemaphoreType.DMA((2, 9)),
            pltpu.SemaphoreType.DMA((2, 9)),
            pltpu.SemaphoreType.DMA((3, experts)),
            pltpu.SemaphoreType.DMA((3, experts)),
        ],
        compiler_params=pltpu.CompilerParams(
            collective_id=0, has_side_effects=True, vmem_limit_bytes=66_000_000
        ),
    )(expert_ids.T, gates.T, tokens, grad_y, w_in[0], w_out[0])
    results = (grad_in, grad_out, mixed, grad_tokens, grad_gates)
    grad_in, grad_out, mixed, grad_tokens, grad_gates = pl.pallas_call(
        place,
        name="place",
        out_shape=tuple(jax.ShapeDtypeStruct(r.shape, r.dtype) for r in results),
        in_specs=[hbm] * 5,
        out_specs=(hbm,) * 5,
        scratch_shapes=[pltpu.VMEM(r.shape, r.dtype) for r in results]
        + [pltpu.SemaphoreType.DMA((5,)), pltpu.SemaphoreType.DMA((5,))],
    )(*results)
    return mixed, grad_tokens, grad_in[None], grad_out[None], grad_gates.T


def solution(mesh):
    return jax.shard_map(
        shards,
        mesh=mesh,
        in_specs=(
            P(("exp", "fsdp"), None),
            P(("exp", "fsdp"), None),
            P(("exp", "fsdp"), None),
            P("exp", "fsdp", None),
            P("exp", "fsdp", None),
            P(("exp", "fsdp"), None),
        ),
        out_specs=(
            P(("exp", "fsdp"), None),
            P(("exp", "fsdp"), None),
            P("exp", "fsdp", None),
            P("exp", "fsdp", None),
            P(("exp", "fsdp"), None),
        ),
        check_vma=False,
    )
```

```python
import functools

import jax
import jax.numpy as jnp
from jax import lax
from jax.experimental import pallas as pl
from jax.experimental.pallas import tpu as pltpu
from jax.sharding import PartitionSpec as P

inv_sqrt_two = 0.7071067811865476
inv_sqrt_two_pi = 0.3989422804014327
MESH = pl.DeviceIdType.MESH
SIDE = 4
BF = jnp.bfloat16
F32 = jnp.float32


def dot(left, right, over):
    return lax.dot_general(left, right, (over, ((), ())), preferred_element_type=F32)


def kernel(
    experts,
    ids_row,
    gates_row,
    tokens,
    grad_y,
    w_in,
    w_out,
    mixed,
    grad_tokens,
    grad_in,
    grad_out,
    grad_gates,
    wts,
    parts0,
    parts1,
    relay0,
    full0,
    last0,
    mate1,
    relay1,
    full1,
    raw_tokens,
    raw_grads,
    raw_ids,
    raw_gates,
    sendx,
    recvx,
    backx,
    acc,
    act_s,
    gh_s,
    act_t,
    gh_t,
    load_sem,
    raw_send,
    raw_recv,
    ag_send,
    ag_recv,
    rs_send,
    rs_recv,
    x_send,
    x_recv,
):
    rows, features = tokens.shape
    half = w_in.shape[0] // 2
    cap = sendx.shape[3]
    slots = experts * cap
    group = SIDE * half
    tile = features // 3

    e = lax.axis_index("exp")
    f = lax.axis_index("fsdp")
    z, y = f // SIDE, f % SIDE
    odd = y % 2
    side = y // 2
    toward = 1 - 2 * odd

    def ring(value):
        return (value + SIDE) % SIDE

    first, second = (y, z), (z, y)

    def axis_of(h, i):
        return "yz"[(h + (i is not None)) % 2]

    def step_of(axis, k):
        if axis == "z":
            return 1 if k % 2 == 0 else -1
        return toward if k % 2 == 0 else -toward

    def peer(axis, k):
        step = step_of(axis, k)
        return (e, ring(z + step) * SIDE + y if axis == "z" else z * SIDE + ring(y + step))

    def copy(src, dst, send, recv, to):
        return pltpu.make_async_remote_copy(
            src_ref=src, dst_ref=dst, send_sem=send, recv_sem=recv, device_id=to, device_id_type=MESH
        )

    def held(h, i):
        return ring(y + toward * i) if h == 0 else ring(z - i)

    def weights(h, i, offset, part=None):
        if i is None:
            at = (h, ring(first[h] + offset), second[h])
        else:
            at = (h, held(h, i), ring(second[h] + offset))
        return wts.at[at if part is None else at + (part,)]

    def gather(h, i, k):
        axis = axis_of(h, i)
        region = weights(h, i, 0) if k < 2 else weights(h, i, -step_of(axis, k), k - 2)
        s = k if i is None else 4 + 4 * i + k
        return copy(region, region, ag_send.at[h, s], ag_recv.at[h, s], peer(axis, k))

    def got(h, i, k):
        axis = axis_of(h, i)
        if k < 2:
            region = weights(h, i, -step_of(axis, k) if axis == "z" else step_of(axis, k))
        else:
            region = weights(h, i, 2, k - 2)
        s = k if i is None else 4 + 4 * i + k
        copy(region, region, ag_send.at[h, s], ag_recv.at[h, s], peer(axis, k)).wait_recv()

    def send(h, i):
        gather(h, i, 0).start()
        gather(h, i, 1).start()

    def forward(h, i, k):
        got(h, i, k - 2 if axis_of(h, i) == "z" else 3 - k)
        gather(h, i, k).start()

    def whole(h, i):
        got(h, i, 2)
        got(h, i, 3)

    raws = [
        copy(src, dst, raw_send.at[k], raw_recv.at[k], peer("y", 1))
        for k, (src, dst) in enumerate(
            ((ids_row, raw_ids), (gates_row, raw_gates), (tokens, raw_tokens), (grad_y, raw_grads))
        )
    ]

    def out_copy(line, step):
        to = (e + step) % experts
        return copy(sendx.at[line, to], recvx.at[line, e], x_send.at[line, step], x_recv.at[line, step], (to, f))

    def out_arrival(line, step):
        src = (e + experts - step) % experts
        return copy(sendx.at[line, src], recvx.at[line, src], x_send.at[line, step], x_recv.at[line, step], (src, f))

    def back_copy(step):
        to = (e + step) % experts
        return copy(sendx.at[0, to], backx.at[e], x_send.at[2, step], x_recv.at[2, step], (to, f))

    def back_arrival(step):
        src = (e + experts - step) % experts
        return copy(sendx.at[0, src], backx.at[src], x_send.at[2, step], x_recv.at[2, step], (src, f))

    def ring0(j, k):
        src = (
            parts0.at[j, ring(z + 2), 0],
            parts0.at[j, ring(z + 2), 1],
            parts0.at[j, ring(z + 1)],
            parts0.at[j, ring(z - 1)],
        )[k]
        dst = (relay0.at[j, 0], relay0.at[j, 1], full0.at[j, 0], full0.at[j, 1])[k]
        return copy(src, dst, rs_send.at[0, 4 * j + k], rs_recv.at[0, 4 * j + k], peer("z", k))

    def mate0():
        return copy(parts0.at[1, z], last0, rs_send.at[0, 8], rs_recv.at[0, 8], peer("y", 0))

    def to_mate1(i):
        return copy(parts1.at[i, 1 - odd], mate1.at[i], rs_send.at[1, i], rs_recv.at[1, i], peer("y", 0))

    def ring1(k):
        src = (parts1.at[2, odd, 0], parts1.at[2, odd, 1], parts1.at[3, odd], parts1.at[1, odd])[k]
        dst = (relay1.at[0], relay1.at[1], full1.at[0], full1.at[1])[k]
        return copy(src, dst, rs_send.at[1, 4 + k], rs_recv.at[1, 4 + k], peer("z", k))

    def add(*terms):
        total = terms[0].astype(F32)
        for t in terms[1:]:
            total = total + t.astype(F32)
        return total

    def relay_ring0(j):
        up, down = ring(z + 1), ring(z - 1)
        ring0(j, 0).wait_recv()
        parts0[j, up, 0] = add(parts0[j, up, 0], relay0[j, 0]).astype(BF)
        ring0(j, 1).wait_recv()
        parts0[j, down, 1] = add(parts0[j, down, 1], relay0[j, 1]).astype(BF)
        ring0(j, 2).start()
        ring0(j, 3).start()

    loads = []
    for h in (0, 1):
        for k, w in ((0, w_in), (1, w_out)):
            loads.append(
                pltpu.make_async_copy(
                    w.at[pl.ds(h * half, half)], wts.at[h, first[h], second[h], k], load_sem.at[2 * h + k]
                )
            )
    for c in loads:
        c.start()
    barrier = pltpu.get_barrier_semaphore()
    for step in range(1, experts):
        pl.semaphore_signal(barrier, inc=1, device_id=((e + step) % experts, f), device_id_type=MESH)
    for axis in "yz":
        for k in (0, 1):
            pl.semaphore_signal(barrier, inc=1, device_id=peer(axis, k), device_id_type=MESH)
    for c in loads:
        c.wait()
    pl.semaphore_wait(barrier, experts + 3)

    send(0, None)
    for c in raws:
        c.start()
    send(1, None)
    send(0, 0)
    send(1, 0)

    def slots_of(ids):
        lane = lax.broadcasted_iota(jnp.int32, (16, rows), 0)
        named = [(lane == ids[k : k + 1, :]).astype(F32) for k in (0, 1)]
        before = (
            lax.broadcasted_iota(jnp.int32, (rows, rows), 0) < lax.broadcasted_iota(jnp.int32, (rows, rows), 1)
        ).astype(BF)
        ahead = dot((named[0] + named[1]).astype(BF), before, ((1,), (0,)))
        return [
            ids[k : k + 1, :].astype(F32) * cap + jnp.sum(named[k] * ahead, axis=0, keepdims=True) for k in (0, 1)
        ]

    def chosen(slot, start, count):
        at = lax.broadcasted_iota(jnp.int32, (count, rows), 0) + start
        return (at.astype(F32) == slot).astype(F32)

    def dispatch(line, ids, gates, patch, cotangent):
        slot = slots_of(ids)

        def fill(d, carry):
            pick = [chosen(slot[k], d * cap, cap) for k in (0, 1)]
            either = (pick[0] + pick[1]).astype(BF)
            gate = jnp.sum(pick[0] * gates[0:1, :] + pick[1] * gates[1:2, :], axis=1, keepdims=True)
            sendx[line, d, 0] = dot(either, patch[...], ((1,), (0,))).astype(BF)
            sendx[line, d, 1] = (dot(either, cotangent[...], ((1,), (0,))) * gate).astype(BF)
            return carry

        lax.fori_loop(0, experts, fill, 0)
        for step in range(1, experts):
            out_copy(line, step).start()
        recvx[line, e] = sendx[line, e]

    dispatch(0, ids_row, gates_row, tokens, grad_y)

    forward(0, None, 3)
    send(0, 1)
    forward(0, None, 2)
    send(0, 3)
    forward(1, None, 2)
    send(1, 1)
    forward(1, None, 3)
    send(1, 3)
    forward(0, 0, 2)
    forward(0, 0, 3)
    forward(1, 0, 3)
    whole(1, None)
    send(1, 2)
    for c in raws:
        c.wait_recv()
    dispatch(1, raw_ids, raw_gates, raw_tokens, raw_grads)
    forward(0, 1, 2)
    forward(0, 1, 3)
    whole(0, None)
    send(0, 2)
    forward(0, 3, 2)
    forward(0, 3, 3)
    acc[...] = jnp.zeros_like(acc)
    for step in range(1, experts):
        out_arrival(0, step).wait_recv()

    def gelu(pre):
        cdf = 0.5 * (1.0 + lax.erf(pre * inv_sqrt_two))
        return pre * cdf, cdf + pre * jnp.exp(-0.5 * pre * pre) * inv_sqrt_two_pi

    def results(h, i):
        g = (1 - h) * ring(y + toward * i) + h * ring(z - i)

        def weight(k, *at):
            return wts[(h, g, slice(None), k, slice(None)) + at].reshape(group, -1)

        def patches(k):
            return recvx[0, :, k].reshape(slots, features)

        act, slope = gelu(dot(patches(0), weight(0), ((1,), (1,))))
        act_s[...] = act.astype(BF)
        gh_s[...] = (dot(patches(1), weight(1), ((1,), (1,))) * slope).astype(BF)

        def columns(c, inner):
            at = pl.ds(pl.multiple_of(c * tile, tile), tile)
            acc[0, :, at] += dot(act_s[...], weight(1, at), ((1,), (0,)))
            acc[1, :, at] += dot(gh_s[...], weight(0, at), ((1,), (0,)))
            return inner

        lax.fori_loop(0, 3, columns, 0)

    def gradients(h, q):
        def weight(k, at):
            if h == 0:
                return wts[0, held(0, q), :, k, :, at].reshape(group, -1)
            pair = [wts[1, held(1, i), pl.ds(2 * side, 2), k, :, at].reshape(group // 2, -1) for i in (q, q + 1)]
            return jnp.concatenate(pair, axis=0)

        every = slice(None)

        def line_of(line, inner):
            act, slope = gelu(dot(recvx[line, :, 0].reshape(slots, features), weight(0, every), ((1,), (1,))))
            hidden = dot(recvx[line, :, 1].reshape(slots, features), weight(1, every), ((1,), (1,))) * slope
            at = pl.ds(pl.multiple_of(line * slots, slots), slots)
            act_t[:, at] = act.T.astype(BF)
            gh_t[:, at] = hidden.T.astype(BF)
            return inner

        lax.fori_loop(0, 2, line_of, 0)

        def columns(c, inner):
            at = pl.ds(pl.multiple_of(c * tile, tile), tile)
            for k, left in ((0, gh_t), (1, act_t)):
                part = dot(left[...], recvx[:, :, k, :, at].reshape(2 * slots, tile), ((1,), (0,))).astype(BF)
                if h == 0:
                    parts0[q, :, k, :, at] = part.reshape(SIDE, half, tile)
                else:
                    parts1[pl.ds(q, 2), :, k, :, at] = part.reshape(2, 2, half, tile)
            return inner

        lax.fori_loop(0, 3, columns, 0)

    def first_results(it, power):
        @pl.when(it == 0)
        def _():
            whole(0, 0)

        @pl.when(it == 1)
        def _():
            forward(1, 0, 2)
            whole(0, 1)

        @pl.when(it == 2)
        def _():
            forward(1, 1, 3)
            forward(0, 2, 2)
            forward(0, 2, 3)
            whole(0, 3)

        results(0, (0o310 // power) % 8)
        return power * 8

    lax.fori_loop(0, 3, first_results, 1)

    forward(1, 1, 2)
    forward(1, 3, 3)
    forward(1, 2, 3)
    for step in range(1, experts):
        out_arrival(1, step).wait_recv()
    forward(1, 3, 2)
    gradients(1, 2)
    to_mate1(2).start()
    to_mate1(3).start()
    gradients(1, 0)
    gradients(0, 1)
    ring0(1, 0).start()
    ring0(1, 1).start()
    forward(1, 2, 2)
    to_mate1(1).start()
    to_mate1(0).start()
    gradients(0, 0)
    ring0(0, 0).start()
    ring0(0, 1).start()

    def last_results(it, power):
        @pl.when(it == 0)
        def _():
            whole(0, 2)
            to_mate1(2).wait_recv()
            parts1[2, odd] = add(parts1[2, odd], mate1[2]).astype(BF)

        @pl.when(it == 1)
        def _():
            ring1(0).start()
            ring1(1).start()
            relay_ring0(1)
            whole(1, 0)

        @pl.when(it == 2)
        def _():
            relay_ring0(0)
            whole(1, 1)

        @pl.when(it == 3)
        def _():
            whole(1, 3)

        @pl.when(it == 4)
        def _():
            whole(1, 2)

        results((0o11110 // power) % 8, (0o23102 // power) % 8)
        return power * 8

    lax.fori_loop(0, 5, last_results, 1)

    for step in range(1, experts):
        out_copy(0, step).wait_send()
    for d in range(experts):
        for k in (0, 1):
            sendx[0, d, k] = acc[k, d * cap : (d + 1) * cap, :].astype(BF)
    for step in range(1, experts):
        back_copy(step).start()
    backx[e] = sendx[0, e]

    to_mate1(3).wait_recv()
    to_mate1(1).wait_recv()
    ring1(0).wait_recv()
    ring1(1).wait_recv()
    parts1[3, odd, 0] = add(parts1[3, odd, 0], mate1[3, 0], relay1[0]).astype(BF)
    parts1[3, odd, 1] = add(parts1[3, odd, 1], mate1[3, 1]).astype(BF)
    parts1[1, odd, 0] = add(parts1[1, odd, 0], mate1[1, 0]).astype(BF)
    parts1[1, odd, 1] = add(parts1[1, odd, 1], mate1[1, 1], relay1[1]).astype(BF)
    ring1(2).start()
    ring1(3).start()
    ring0(1, 2).wait_recv()
    ring0(1, 3).wait_recv()
    parts0[1, z] = add(parts0[1, z], full0[1, 0], full0[1, 1]).astype(BF)
    mate0().start()

    to_mate1(0).wait_recv()
    ring1(2).wait_recv()
    ring1(3).wait_recv()
    for part, out in ((0, grad_in), (1, grad_out)):
        out[half : 2 * half, :] = add(
            parts1[0, odd, part], mate1[0, part], full1[0, part], full1[1, part]
        )
    ring0(0, 2).wait_recv()
    ring0(0, 3).wait_recv()
    mate0().wait_recv()
    for part, out in ((0, grad_in), (1, grad_out)):
        out[0:half, :] = add(parts0[0, z, part], full0[0, 0, part], full0[0, 1, part], last0[part])

    for step in range(1, experts):
        back_arrival(step).wait_recv()
    slot = slots_of(ids_row)
    pick = [chosen(slot[k], 0, slots).astype(BF) for k in (0, 1)]
    both = pick[0] + pick[1]
    square = (rows, rows)
    diagonal = (
        lax.broadcasted_iota(jnp.int32, square, 0) == lax.broadcasted_iota(jnp.int32, square, 1)
    ).astype(F32)
    gate_col = [jnp.sum(diagonal * gates_row[k : k + 1, :], axis=1, keepdims=True) for k in (0, 1)]
    by_gate = [jnp.zeros((rows, 1), F32) for _ in (0, 1)]
    for c in range(3):
        at = slice(c * tile, (c + 1) * tile)
        outs = backx[:, 0, :, at].reshape(slots, tile)
        grads = backx[:, 1, :, at].reshape(slots, tile)
        cot = grad_y[:, at].astype(F32)
        total = jnp.zeros((rows, tile), F32)
        for k in (0, 1):
            one = dot(pick[k], outs, ((0,), (0,)))
            total = total + gate_col[k] * one
            by_gate[k] = by_gate[k] + jnp.sum(cot * one, axis=1, keepdims=True)
        mixed[:, at] = total.astype(BF)
        grad_tokens[:, at] = dot(both, grads, ((0,), (0,))).astype(BF)
    for k in (0, 1):
        grad_gates[k : k + 1, :] = jnp.sum(diagonal * by_gate[k], axis=0, keepdims=True)

    for c in raws:
        c.wait_send()
    for step in range(1, experts):
        out_copy(1, step).wait_send()
        back_copy(step).wait_send()
    mate0().wait_send()
    for k in range(4):
        to_mate1(k).wait_send()
        ring1(k).wait_send()
        for j in (0, 1):
            ring0(j, k).wait_send()
        for h in (0, 1):
            for i in (None, 0, 1, 2, 3):
                gather(h, i, k).wait_send()


def place(*refs):
    given, taken, held, (into, outof) = refs[:5], refs[5:10], refs[10:15], refs[15:]
    ins = [pltpu.make_async_copy(given[k], held[k], into.at[k]) for k in range(5)]
    outs = [pltpu.make_async_copy(held[k], taken[k], outof.at[k]) for k in range(5)]
    for c in ins:
        c.start()
    for k in range(5):
        ins[k].wait()
        outs[k].start()
    for c in outs:
        c.wait()


def shards(tokens, expert_ids, gates, w_in, w_out, grad_y):
    rows, features = tokens.shape
    experts = lax.axis_size("exp")
    cap = 3 * rows // 8
    hidden = w_in.shape[1]
    half = hidden // 2
    group = SIDE * half
    slots = experts * cap
    vmem = pl.BlockSpec(memory_space=pltpu.VMEM)
    hbm = pl.BlockSpec(memory_space=pl.ANY)
    mixed, grad_tokens, grad_in, grad_out, grad_gates = pl.pallas_call(
        functools.partial(kernel, experts),
        name="moe",
        out_shape=(
            jax.ShapeDtypeStruct((rows, features), BF),
            jax.ShapeDtypeStruct((rows, features), BF),
            jax.ShapeDtypeStruct((hidden, features), F32),
            jax.ShapeDtypeStruct((hidden, features), F32),
            jax.ShapeDtypeStruct((2, rows), F32),
        ),
        in_specs=[vmem] * 4 + [hbm] * 2,
        out_specs=(vmem,) * 5,
        scratch_shapes=[
            pltpu.VMEM((2, SIDE, SIDE, 2, half, features), BF),
            pltpu.VMEM((2, SIDE, 2, half, features), BF),
            pltpu.VMEM((SIDE, 2, 2, half, features), BF),
            pltpu.VMEM((2, 2, half, features), BF),
            pltpu.VMEM((2, 2, 2, half, features), BF),
            pltpu.VMEM((2, half, features), BF),
            pltpu.VMEM((SIDE, 2, half, features), BF),
            pltpu.VMEM((2, half, features), BF),
            pltpu.VMEM((2, 2, half, features), BF),
            pltpu.VMEM((rows, features), BF),
            pltpu.VMEM((rows, features), BF),
            pltpu.VMEM((2, rows), jnp.int32),
            pltpu.VMEM((2, rows), F32),
            pltpu.VMEM((2, experts, 2, cap, features), BF),
            pltpu.VMEM((2, experts, 2, cap, features), BF),
            pltpu.VMEM((experts, 2, cap, features), BF),
            pltpu.VMEM((2, slots, features), F32),
            pltpu.VMEM((slots, group), BF),
            pltpu.VMEM((slots, group), BF),
            pltpu.VMEM((group, 2 * slots), BF),
            pltpu.VMEM((group, 2 * slots), BF),
            pltpu.SemaphoreType.DMA((4,)),
            pltpu.SemaphoreType.DMA((4,)),
            pltpu.SemaphoreType.DMA((4,)),
            pltpu.SemaphoreType.DMA((2, 20)),
            pltpu.SemaphoreType.DMA((2, 20)),
            pltpu.SemaphoreType.DMA((2, 9)),
            pltpu.SemaphoreType.DMA((2, 9)),
            pltpu.SemaphoreType.DMA((3, experts)),
            pltpu.SemaphoreType.DMA((3, experts)),
        ],
        compiler_params=pltpu.CompilerParams(
            collective_id=0, has_side_effects=True, vmem_limit_bytes=66_000_000
        ),
    )(expert_ids.T, gates.T, tokens, grad_y, w_in[0], w_out[0])
    results = (grad_in, grad_out, mixed, grad_tokens, grad_gates)
    grad_in, grad_out, mixed, grad_tokens, grad_gates = pl.pallas_call(
        place,
        name="place",
        out_shape=tuple(jax.ShapeDtypeStruct(r.shape, r.dtype) for r in results),
        in_specs=[hbm] * 5,
        out_specs=(hbm,) * 5,
        scratch_shapes=[pltpu.VMEM(r.shape, r.dtype) for r in results]
        + [pltpu.SemaphoreType.DMA((5,)), pltpu.SemaphoreType.DMA((5,))],
    )(*results)
    return mixed, grad_tokens, grad_in[None], grad_out[None], grad_gates.T


def solution(mesh):
    return jax.shard_map(
        shards,
        mesh=mesh,
        in_specs=(
            P(("exp", "fsdp"), None),
            P(("exp", "fsdp"), None),
            P(("exp", "fsdp"), None),
            P("exp", "fsdp", None),
            P("exp", "fsdp", None),
            P(("exp", "fsdp"), None),
        ),
        out_specs=(
            P(("exp", "fsdp"), None),
            P(("exp", "fsdp"), None),
            P("exp", "fsdp", None),
            P("exp", "fsdp", None),
            P(("exp", "fsdp"), None),
        ),
        check_vma=False,
    )
```
